32 devices in a mesh: kgrp: 4 (over x, core), band: 8 (over z, y).
Axes of the slice: x: 2, y: 2, z: 4, core: 2. Of those that a mesh axis runs over, the one named last changes fastest.
Arguments:
- densities: bfloat16 [8, 128, 128, 4096], P('kgrp', 'band'), may hold values from -6 to 6
- amplitudes: bfloat16 [8, 8, 128, 128], P('kgrp'), may hold values from -0.046875 to 0.046875
- partner: int32 [8], replicated, may hold values from 0 to 7, as said below
- qtable: int32 [8], replicated, may hold values from 0 to 63
- grid_map: int32 [64, 4096], replicated, may hold values from 0 to 4095, each once within a row
- coulomb: float32 [64, 4096], replicated, may hold values from 0.5 to 2
Outputs:
- ladder: bfloat16 [128, 8, 8, 128], P('band', 'kgrp')
The draws below stay inside these ranges and needn't reach their ends.
Inputs may be any that keep to these rules, and one draw needn't show every extreme that they name: partner is a permutation of the 8 k-pairs; k-pair r lies in group r // 2. The two pairs of a group have their partners in two different groups, neither of them the group itself, and the two pairs whose partners lie in one group belong to two different groups. `grid_map`: each row is a permutation of the 4096 grid positions.
All inputs are finite; a program needn't handle non-finite values.
Results may differ from the reference program's by a relative error of at most 0.0064.
Values may be sent and summed in bfloat16 or wider, within the bound.
A program may use at most 448 MiB of HBM per device.

```python
import math
import jax
import jax.numpy as jnp
from jax import lax

VB = 128
G = 4096
NQ = 64
IJ = 8
NK = 8


def draw_partner(key, part):
    groups = NK // 2
    first_shift = jax.random.randint(jax.random.fold_in(key, 21), (), 1, groups)
    offset = jax.random.randint(jax.random.fold_in(key, 22), (), 0, groups - 2)
    second_shift = (first_shift + offset) % (groups - 1) + 1
    sender_bit = jax.random.randint(jax.random.fold_in(key, 23), (groups,), 0, 2)
    receiver_bit = jax.random.randint(jax.random.fold_in(key, 24), (groups,), 0, 2)
    group_ids = jnp.arange(groups, dtype=jnp.int32)
    first_dest = (group_ids + first_shift) % groups
    second_dest = (group_ids + second_shift) % groups
    first_target = 2 * first_dest + receiver_bit[first_dest]
    second_target = 2 * second_dest + 1 - receiver_bit[second_dest]
    slot_zero = jnp.where(sender_bit == 0, first_target, second_target)
    slot_one = jnp.where(sender_bit == 0, second_target, first_target)
    return jnp.stack([slot_zero, slot_one], axis=1).reshape(NK).astype(jnp.int32)


def with_ends(entries, key, low, largest):
    place = [jax.random.randint(jax.random.fold_in(key, axis), (), 0, length) for axis, length in enumerate(entries.shape)]
    main_axis = entries.shape.index(max(entries.shape))
    beside = place[:main_axis] + [(place[main_axis] + 1) % entries.shape[main_axis]] + place[main_axis + 1:]
    return entries.at[tuple(place)].set(low).at[tuple(beside)].set(largest)


def spiked(entries, own_key, source, target, blocks, factor):
    owner, partner = [(jnp.arange(entries.shape[axis_at]) // (entries.shape[axis_at] // blocks)).reshape([-1 if axis == axis_at else 1 for axis in range(entries.ndim)]) for axis_at in (source, target)]
    chosen = jax.random.permutation(own_key, blocks)[partner]
    strong = (owner == chosen) | (owner == (partner + blocks // 2) % blocks)
    return jnp.where(strong, factor * entries, entries)


def block_levels(stream_key, extent, shards, least, top_value):
    def one(axis_at, blocks):
        draws = jax.random.uniform(jax.random.fold_in(jax.random.fold_in(stream_key, 6), axis_at), (blocks,), jnp.float32, least / len(shards), top_value / len(shards))
        return jnp.repeat(jnp.exp(draws), extent[axis_at] // blocks).reshape((-1,) + (1,) * (len(extent) - axis_at - 1))

    gain = one(*shards[0])
    for cut in shards[1:]:
        gain = gain * one(*cut)
    return gain


def normal_values(stream_key, shape, spread, bound, shards=(), kind=jnp.bfloat16):
    loudness = block_levels(stream_key, shape, shards, -0.22, 0.18) if shards else 1.0
    drawn = jax.random.normal(stream_key, shape, jnp.float32) * spread * loudness
    return jnp.minimum(jnp.maximum(drawn, -bound), bound).astype(kind)


def bell_draw_with(stream_key, extent, scale, reach, cuts, heavy, held_as=jnp.bfloat16):
    array = scale * jax.random.normal(stream_key, extent, jnp.float32)
    if cuts:
        array = array * block_levels(stream_key, extent, cuts, -0.22, 0.18)
    return jnp.clip(spiked(array, jax.random.fold_in(stream_key, 3), *heavy), -reach, reach).astype(held_as)


def setup_inputs(seed: int = 0) -> dict:
    arg_keys = jax.random.split(jax.random.key(seed), 7)
    return {
        "densities": bell_draw_with(arg_keys[0], (NK, VB, VB, G), 1.0, 6.0, ((0, 4), (1, 8)), (3, 1, 8, 2.0)),
        "amplitudes": normal_values(arg_keys[1], (NK, IJ, VB, VB), (VB * VB) ** -0.5, 0.046875, ((0, 4),)),
        "partner": draw_partner(jax.random.fold_in(arg_keys[6], 71), 0),
        "qtable": with_ends(jax.random.randint(arg_keys[3], (NK,), 0, NQ), jax.random.fold_in(arg_keys[3], 1), 0, NQ - 1).astype(jnp.int32),
        "grid_map": jax.vmap(lambda own: jax.random.permutation(own, G))(jax.random.split(arg_keys[4], NQ)).reshape((NQ, G)).astype(jnp.int32),
        "coulomb": jnp.clip(jnp.exp(jax.random.uniform(arg_keys[5], (NQ, G), jnp.float32, math.log(0.5), math.log(2.0))), 0.5, 2.0),
    }


def make_vertex(densities, qtable, grid_map, coulomb, pair_index):
    transfer = qtable[pair_index]
    grid_rows = grid_map[transfer]
    factors = coulomb[transfer]
    picked = jnp.take(densities[pair_index], grid_rows, axis=2)
    return (picked.astype(jnp.float32) * factors[None, None, :]).astype(jnp.bfloat16)

def reference(densities, amplitudes, partner, qtable, grid_map, coulomb):

    def per_pair(pair_index):
        left_block = make_vertex(densities, qtable, grid_map, coulomb, pair_index)
        right_block = make_vertex(densities, qtable, grid_map, coulomb, partner[pair_index])
        left_wide = left_block.astype(jnp.float32)
        right_wide = right_block.astype(jnp.float32)

        def per_slab(amp_pair):
            mixed = jnp.einsum('acg,cd->adg', left_wide, amp_pair.astype(jnp.float32)).astype(jnp.bfloat16)
            return jnp.einsum('adg,bdg->ab', mixed.astype(jnp.float32), right_wide)
        return lax.map(per_slab, amplitudes[pair_index])
    sums = lax.map(per_pair, jnp.arange(NK, dtype=jnp.int32))
    scaled = sums * (1.0 / math.sqrt(G))
    return jnp.transpose(scaled, (2, 0, 1, 3)).astype(jnp.bfloat16)
```

```python
import functools
import math

import jax
import jax.numpy as jnp
from jax import lax
from jax.experimental import pallas as pl
from jax.experimental.pallas import tpu as pltpu
from jax.sharding import PartitionSpec as P

MESH = pl.DeviceIdType.MESH
SLOTS = 3
DEPTH = 4


def fused_kernel(
    kgrp, band, partner_ref, index_ref, factor_ref, densities_ref, amplitudes_ref,
    recv_ref, out_ref,
    turned, staged, slots, block, amps, total,
    turn_sem, send_sem, recv_sem, amp_send, amp_recv, load_sem,
):
    devices = kgrp * band
    per_group, rows, width, g_all = densities_ref.shape
    rows_by_g = turned.reshape(per_group * g_all, rows, width)
    chunks = recv_ref.shape[0]
    depth = slots.shape[3]
    slabs = amps.shape[1]
    g_shard = chunks * depth
    pairs = kgrp * per_group
    vb = band * rows
    my_k, my_b = lax.axis_index("kgrp"), lax.axis_index("band")
    me = my_k * band + my_b

    def peer(m):
        return lax.rem(my_k + lax.rem(m, kgrp), kgrp), lax.rem(my_b + m // kgrp, band)

    barrier = pltpu.get_barrier_semaphore()

    def greet(m, carry):
        pl.semaphore_signal(barrier, inc=1, device_id=peer(m), device_id_type=MESH)
        return carry

    lax.fori_loop(1, devices, greet, 0)
    pl.semaphore_wait(barrier, devices - 1)

    span = staged.shape[-1]
    steps = g_all // span

    def fetch(p, i):
        return pltpu.make_async_copy(
            densities_ref.at[p, :, :, pl.ds(pl.multiple_of(i * span, span), span)],
            staged.at[lax.rem(i, 2)],
            turn_sem.at[lax.rem(i, 2)],
        )

    def turn(p):
        fetch(p, 0).start()

        def one(i, carry):
            @pl.when(i + 1 < steps)
            def _():
                fetch(p, i + 1).start()

            fetch(p, i).wait()
            flat = staged[lax.rem(i, 2)].reshape(rows * width, span)
            turned[p * steps + i] = flat.T.reshape(span, rows, width)
            return carry

        lax.fori_loop(0, steps, one, 0)

    def pick(p, chunk):
        slot = lax.rem(chunk, SLOTS)

        def one(d, carry):
            first = d * g_shard + chunk * depth
            for j in range(depth):
                row = rows_by_g[p * g_all + index_ref[p, first + j]].astype(jnp.float32) * factor_ref[p, first + j]
                slots[slot, d, p, j] = row.astype(slots.dtype)
            return carry

        lax.fori_loop(0, devices, one, 0, unroll=2)

    def send(chunk, piece):
        slot = lax.rem(chunk, SLOTS)

        def one(m, carry):
            to_k, to_b = peer(m)
            pltpu.make_async_remote_copy(
                src_ref=piece(slots.at[slot, to_k * band + to_b]),
                dst_ref=piece(recv_ref.at[chunk, me]),
                send_sem=send_sem.at[slot],
                recv_sem=recv_sem.at[chunk],
                device_id=(to_k, to_b),
                device_id_type=MESH,
            ).start()
            return carry

        lax.fori_loop(1, devices, one, 0)
        pltpu.make_async_copy(piece(slots.at[slot, me]), piece(recv_ref.at[chunk, me]), send_sem.at[slot]).start()

    def ladder(chunk):
        others = pl.ds(0, devices - 1)
        pltpu.make_async_copy(
            recv_ref.at[chunk, others], recv_ref.at[chunk, others], recv_sem.at[chunk]
        ).wait()
        load = pltpu.make_async_copy(recv_ref.at[chunk], block, load_sem)
        load.start()
        load.wait()

        def one(r, carry):
            q = partner_ref[r]
            left_base, left_pair = r // per_group * band, lax.rem(r, per_group)
            right_base, right_pair = q // per_group * band, lax.rem(q, per_group)
            left = jnp.concatenate(
                [block[left_base + b, left_pair, j] for j in range(depth) for b in range(band)], axis=0
            )
            right = jnp.concatenate(
                [
                    jnp.concatenate([block[right_base + b, right_pair, j] for b in range(band)], axis=0)
                    for j in range(depth)
                ],
                axis=1,
            )
            amp = jnp.concatenate([amps[r, s] for s in range(slabs)], axis=1)
            mixed = jnp.dot(left, amp, preferred_element_type=jnp.float32).astype(jnp.bfloat16)
            wide = jnp.concatenate(
                [
                    jnp.concatenate(
                        [mixed[j * vb:(j + 1) * vb, s * width:(s + 1) * width] for j in range(depth)], axis=1
                    )
                    for s in range(slabs)
                ],
                axis=0,
            )
            total[r] += lax.dot_general(wide, right, (((1,), (1,)), ((), ())), preferred_element_type=jnp.float32)
            return carry

        lax.fori_loop(0, pairs, one, 0)

    def amp_copy(m):
        to_k = lax.rem(my_k + m, kgrp)
        return pltpu.make_async_remote_copy(
            src_ref=amplitudes_ref,
            dst_ref=amps.at[pl.ds(my_k * per_group, per_group)],
            send_sem=amp_send,
            recv_sem=amp_recv,
            device_id=(to_k, my_b),
            device_id_type=MESH,
        )

    own_amp = pltpu.make_async_copy(amplitudes_ref, amps.at[pl.ds(my_k * per_group, per_group)], load_sem)

    def begin(p, carry):
        turn(p)
        for chunk in range(SLOTS):
            pick(p, chunk)
            if chunk:
                send(chunk - 1, lambda ref: ref.at[p])
        send(SLOTS - 1, lambda ref: ref.at[p])
        return carry

    total[...] = jnp.zeros_like(total)
    lax.fori_loop(0, per_group, begin, 0)
    own_amp.start()
    for m in range(1, kgrp):
        amp_copy(m).start()
    own_amp.wait()
    all_amps = amps.at[pl.ds(0, (kgrp - 1) * per_group)]
    pltpu.make_async_copy(all_amps, all_amps, amp_send).wait()
    pltpu.make_async_copy(all_amps, all_amps, amp_recv).wait()

    def main(chunk, carry):
        slot = lax.rem(chunk, SLOTS)
        pltpu.make_async_copy(slots.at[slot], slots.at[slot], send_sem.at[slot]).wait()

        @pl.when(chunk < chunks)
        def _():
            for p in range(per_group):
                pick(p, chunk)

        ladder(chunk - SLOTS)

        @pl.when(chunk < chunks)
        def _():
            send(chunk, lambda ref: ref)

        return carry

    lax.fori_loop(SLOTS, chunks + SLOTS, main, 0)
    out_ref[...] = total[...].astype(out_ref.dtype)


def fused(kgrp, band, densities, amplitudes, partner, index, factors):
    per_group, rows, width, g_all = densities.shape
    slabs = amplitudes.shape[1]
    devices = kgrp * band
    pairs = kgrp * per_group
    vb = rows * band
    g_shard = g_all // devices
    depth = math.gcd(g_shard, DEPTH)
    chunks = g_shard // depth
    span = math.gcd(g_all, 256)
    kind = densities.dtype
    anywhere = pl.BlockSpec(memory_space=pl.ANY)
    scalars = pl.BlockSpec(memory_space=pltpu.SMEM)
    piece = (per_group, depth, rows, width)
    return pl.pallas_call(
        functools.partial(fused_kernel, kgrp, band),
        in_specs=[scalars, scalars, scalars, anywhere, anywhere],
        out_specs=[anywhere, pl.BlockSpec(memory_space=pltpu.VMEM)],
        out_shape=[
            jax.ShapeDtypeStruct((chunks, devices) + piece, kind),
            jax.ShapeDtypeStruct((pairs, slabs * vb, vb), kind),
        ],
        scratch_shapes=[
            pltpu.VMEM((per_group * g_all // span, span, rows, width), kind),
            pltpu.VMEM((2, rows, width, span), kind),
            pltpu.VMEM((SLOTS, devices) + piece, kind),
            pltpu.VMEM((devices,) + piece, kind),
            pltpu.VMEM((pairs,) + amplitudes.shape[1:], kind),
            pltpu.VMEM((pairs, slabs * vb, vb), jnp.float32),
            pltpu.SemaphoreType.DMA((2,)),
            pltpu.SemaphoreType.DMA((SLOTS,)),
            pltpu.SemaphoreType.DMA((chunks,)),
            pltpu.SemaphoreType.DMA,
            pltpu.SemaphoreType.DMA,
            pltpu.SemaphoreType.DMA,
        ],
        compiler_params=pltpu.CompilerParams(
            collective_id=0, has_side_effects=True, vmem_limit_bytes=62 * 1024 * 1024
        ),
        name="fused",
    )(partner, index, factors, densities, amplitudes)


def shards(kgrp, band, densities, amplitudes, partner, qtable, grid_map, coulomb):
    per_group, rows, width, g_all = densities.shape
    slabs = amplitudes.shape[1]
    vb = rows * band
    devices = kgrp * band
    own_ids = lax.axis_index("kgrp") * per_group + jnp.arange(per_group, dtype=jnp.int32)
    transfers = jnp.take(qtable, own_ids)
    index = jnp.take(grid_map, transfers, axis=0)
    factors = jnp.take(coulomb, transfers, axis=0)
    _, sums = fused(kgrp, band, densities, amplitudes, partner, index, factors)
    sums = sums.reshape(kgrp, per_group, slabs, band, rows, vb)
    sums = jnp.transpose(sums, (0, 3, 1, 2, 4, 5)).reshape(devices, per_group, slabs, rows, vb)
    sums = lax.all_to_all(sums, ("kgrp", "band"), split_axis=0, concat_axis=0, tiled=True)
    summed = jnp.sum(sums.astype(jnp.float32), axis=0) * (1.0 / math.sqrt(g_all))
    return jnp.transpose(summed, (2, 0, 1, 3)).astype(jnp.bfloat16)


def solution(mesh):
    in_specs = (P("kgrp", "band", None, None), P("kgrp", None, None, None), P(), P(), P(), P())
    out_specs = P("band", "kgrp", None, None)
    body = functools.partial(shards, mesh.shape["kgrp"], mesh.shape["band"])
    return jax.shard_map(body, mesh=mesh, in_specs=in_specs, out_specs=out_specs, check_vma=False)
```

```python
import functools
import math

import jax
import jax.numpy as jnp
from jax import lax
from jax.experimental import pallas as pl
from jax.experimental.pallas import tpu as pltpu
from jax.sharding import PartitionSpec as P

MESH = pl.DeviceIdType.MESH
SLOTS = 3
DEPTH = 4


def fused_kernel(
    kgrp, band, partner_ref, index_ref, factor_ref, densities_ref, amplitudes_ref,
    recv_ref, out_ref,
    turned, staged, slots, block, amps, total,
    core_out, core_in, chip_out, chip_in, far_out, far_in,
    turn_sem, send_sem, recv_sem, amp_send, amp_recv, load_sem,
    core_sent, core_came, chip_sent, chip_came, far_sent, far_came,
):
    devices = kgrp * band
    per_group, rows, width, g_all = densities_ref.shape
    rows_by_g = turned.reshape(per_group * g_all, rows, width)
    chunks = recv_ref.shape[0]
    depth = slots.shape[3]
    slabs = amps.shape[1]
    g_shard = chunks * depth
    pairs = kgrp * per_group
    vb = band * rows
    my_k, my_b = lax.axis_index("kgrp"), lax.axis_index("band")
    me = my_k * band + my_b
    near_k, near_b = math.gcd(kgrp, 2), math.gcd(band, 2)
    wide_k, wide_b = kgrp // near_k, band // near_b
    my_x, my_c = my_k // near_k, lax.rem(my_k, near_k)
    my_z, my_y = my_b // near_b, lax.rem(my_b, near_b)
    half = wide_k * per_group
    away = (near_k - 1) * half

    def peer(m):
        return lax.rem(my_k + lax.rem(m, kgrp), kgrp), lax.rem(my_b + m // kgrp, band)

    barrier = pltpu.get_barrier_semaphore()

    def greet(m, carry):
        pl.semaphore_signal(barrier, inc=1, device_id=peer(m), device_id_type=MESH)
        return carry

    lax.fori_loop(1, devices, greet, 0)
    pl.semaphore_wait(barrier, devices - 1)

    span = staged.shape[-1]
    steps = g_all // span

    def fetch(p, i):
        return pltpu.make_async_copy(
            densities_ref.at[p, :, :, pl.ds(pl.multiple_of(i * span, span), span)],
            staged.at[lax.rem(i, 2)],
            turn_sem.at[lax.rem(i, 2)],
        )

    def turn(p):
        fetch(p, 0).start()

        def one(i, carry):
            @pl.when(i + 1 < steps)
            def _():
                fetch(p, i + 1).start()

            fetch(p, i).wait()
            flat = staged[lax.rem(i, 2)].reshape(rows * width, span)
            turned[p * steps + i] = flat.T.reshape(span, rows, width)
            return carry

        lax.fori_loop(0, steps, one, 0)

    def pick(p, chunk):
        slot = lax.rem(chunk, SLOTS)

        def one(d, carry):
            first = d * g_shard + chunk * depth
            for j in range(depth):
                row = rows_by_g[p * g_all + index_ref[p, first + j]].astype(jnp.float32) * factor_ref[p, first + j]
                slots[slot, d, p, j] = row.astype(slots.dtype)
            return carry

        lax.fori_loop(0, devices, one, 0, unroll=2)

    def send(chunk, piece):
        slot = lax.rem(chunk, SLOTS)

        def one(m, carry):
            to_k, to_b = peer(m)
            pltpu.make_async_remote_copy(
                src_ref=piece(slots.at[slot, to_k * band + to_b]),
                dst_ref=piece(recv_ref.at[chunk, me]),
                send_sem=send_sem.at[slot],
                recv_sem=recv_sem.at[chunk],
                device_id=(to_k, to_b),
                device_id_type=MESH,
            ).start()
            return carry

        lax.fori_loop(1, devices, one, 0)
        pltpu.make_async_copy(piece(slots.at[slot, me]), piece(recv_ref.at[chunk, me]), send_sem.at[slot]).start()

    def core_copy(r, step_c, order, to_c):
        at = step_c - 1
        core_out[at, order] = total[r].astype(core_out.dtype)
        pltpu.make_async_remote_copy(
            src_ref=core_out.at[at, order],
            dst_ref=core_in.at[at, order],
            send_sem=core_sent,
            recv_sem=core_came.at[order],
            device_id=(my_x * near_k + to_c, my_b),
            device_id_type=MESH,
        ).start()

    def chip_copies(r, step_x, order, pair, to_x):
        if near_k > 1:
            came = core_in.at[:, order]
            pltpu.make_async_copy(came, came, core_came.at[order]).wait()
        for step_y in range(near_b):
            to_y = lax.rem(my_y + step_y, near_b)
            value = total[r, :, :, to_y]
            for at in range(near_k - 1):
                value = value + core_in[at, order, :, :, to_y].astype(jnp.float32)

            def leave(value=value, step_y=step_y, to_y=to_y):
                chip_out[order, step_y] = value.astype(chip_out.dtype)
                pltpu.make_async_remote_copy(
                    src_ref=chip_out.at[order, step_y],
                    dst_ref=chip_in.at[pair, step_x * near_b + step_y - 1],
                    send_sem=chip_sent,
                    recv_sem=chip_came.at[pair],
                    device_id=(to_x * near_k + my_c, my_z * near_b + to_y),
                    device_id_type=MESH,
                ).start()

            def keep(value=value, to_y=to_y):
                total[r, :, :, to_y] = value

            if step_y:
                leave()
            else:
                pl.when(step_x > 0)(leave)
                pl.when(step_x == 0)(keep)

    def finish():
        own = [my_k * per_group + pair for pair in range(per_group)]
        peers = wide_k * near_b - 1

        def gathered(pair, z):
            value = total[own[pair], :, z, my_y]
            for at in range(peers):
                value = value + chip_in[pair, at, :, z].astype(jnp.float32)
            return value

        for pair in range(per_group):
            if peers:
                pltpu.make_async_copy(chip_in.at[pair], chip_in.at[pair], chip_came.at[pair]).wait()

            def one(step, carry, pair=pair):
                to_z = lax.rem(my_z + step, wide_b)
                far_out[pair, step - 1] = gathered(pair, to_z).astype(far_out.dtype)
                pltpu.make_async_remote_copy(
                    src_ref=far_out.at[pair, step - 1],
                    dst_ref=far_in.at[pair, step - 1],
                    send_sem=far_sent,
                    recv_sem=far_came.at[pair],
                    device_id=(my_k, to_z * near_b + my_y),
                    device_id_type=MESH,
                ).start()
                return carry

            lax.fori_loop(1, wide_b, one, 0)
        for pair in range(per_group):
            value = gathered(pair, my_z)
            if wide_b > 1:
                pltpu.make_async_copy(far_in.at[pair], far_in.at[pair], far_came.at[pair]).wait()
            for at in range(wide_b - 1):
                value = value + far_in[pair, at].astype(jnp.float32)
            value = value * (1.0 / math.sqrt(g_all))
            out_ref[:, pair] = jnp.swapaxes(value, 0, 1).astype(out_ref.dtype)
        if near_k > 1:
            pltpu.make_async_copy(core_out, core_out, core_sent).wait()
        for order in range(half):
            for step_y in range(near_b):
                if step_y or order < half - per_group:
                    sent = chip_out.at[order, step_y]
                    pltpu.make_async_copy(sent, sent, chip_sent).wait()
        if wide_b > 1:
            pltpu.make_async_copy(far_out, far_out, far_sent).wait()

    def ladder(chunk):
        others = pl.ds(0, devices - 1)
        pltpu.make_async_copy(
            recv_ref.at[chunk, others], recv_ref.at[chunk, others], recv_sem.at[chunk]
        ).wait()
        load = pltpu.make_async_copy(recv_ref.at[chunk], block, load_sem)
        load.start()
        load.wait()

        def one(i, carry):
            order = lax.rem(i, half)
            step_c, step_x, pair = near_k - 1 - i // half, wide_k - 1 - order // per_group, lax.rem(order, per_group)
            to_c, to_x = lax.rem(my_c + step_c, near_k), lax.rem(my_x + step_x, wide_k)
            r = (to_x * near_k + to_c) * per_group + pair
            q = partner_ref[r]
            left_base, left_pair = r // per_group * band, lax.rem(r, per_group)
            right_base, right_pair = q // per_group * band, lax.rem(q, per_group)
            left = jnp.concatenate(
                [block[left_base + b, left_pair, j] for j in range(depth) for b in range(band)], axis=0
            )
            right = jnp.concatenate(
                [
                    jnp.concatenate([block[right_base + b, right_pair, j] for b in range(band)], axis=0)
                    for j in range(depth)
                ],
                axis=1,
            )
            amp = jnp.concatenate([amps[r, s] for s in range(slabs)], axis=1)
            mixed = jnp.dot(left, amp, preferred_element_type=jnp.float32).astype(jnp.bfloat16)
            wide = jnp.concatenate(
                [
                    jnp.concatenate(
                        [mixed[j * vb:(j + 1) * vb, s * width:(s + 1) * width] for j in range(depth)], axis=1
                    )
                    for s in range(slabs)
                ],
                axis=0,
            )
            part = lax.dot_general(wide, right, (((1,), (1,)), ((), ())), preferred_element_type=jnp.float32)
            total[r] += part.reshape(slabs, wide_b, near_b, rows, vb)

            @pl.when((chunk == chunks - 1) & (i < away))
            def _():
                core_copy(r, step_c, order, to_c)

            @pl.when((chunk == chunks - 1) & (i >= away))
            def _():
                chip_copies(r, step_x, order, pair, to_x)

            return carry

        lax.fori_loop(0, pairs, one, 0)

    def amp_copy(m):
        to_k = lax.rem(my_k + m, kgrp)
        return pltpu.make_async_remote_copy(
            src_ref=amplitudes_ref,
            dst_ref=amps.at[pl.ds(my_k * per_group, per_group)],
            send_sem=amp_send,
            recv_sem=amp_recv,
            device_id=(to_k, my_b),
            device_id_type=MESH,
        )

    own_amp = pltpu.make_async_copy(amplitudes_ref, amps.at[pl.ds(my_k * per_group, per_group)], load_sem)

    def begin(p, carry):
        turn(p)
        for chunk in range(SLOTS):
            pick(p, chunk)
            if chunk:
                send(chunk - 1, lambda ref: ref.at[p])
        send(SLOTS - 1, lambda ref: ref.at[p])
        return carry

    total[...] = jnp.zeros_like(total)
    lax.fori_loop(0, per_group, begin, 0)
    own_amp.start()
    for m in range(1, kgrp):
        amp_copy(m).start()
    own_amp.wait()
    all_amps = amps.at[pl.ds(0, (kgrp - 1) * per_group)]
    pltpu.make_async_copy(all_amps, all_amps, amp_send).wait()
    pltpu.make_async_copy(all_amps, all_amps, amp_recv).wait()

    def main(chunk, carry):
        slot = lax.rem(chunk, SLOTS)
        pltpu.make_async_copy(slots.at[slot], slots.at[slot], send_sem.at[slot]).wait()

        @pl.when(chunk < chunks)
        def _():
            for p in range(per_group):
                pick(p, chunk)

        ladder(chunk - SLOTS)

        @pl.when(chunk < chunks)
        def _():
            send(chunk, lambda ref: ref)

        return carry

    lax.fori_loop(SLOTS, chunks + SLOTS, main, 0)
    finish()


def fused(kgrp, band, densities, amplitudes, partner, index, factors):
    per_group, rows, width, g_all = densities.shape
    slabs = amplitudes.shape[1]
    devices = kgrp * band
    pairs = kgrp * per_group
    vb = rows * band
    g_shard = g_all // devices
    depth = math.gcd(g_shard, DEPTH)
    chunks = g_shard // depth
    span = math.gcd(g_all, 256)
    kind = densities.dtype
    anywhere = pl.BlockSpec(memory_space=pl.ANY)
    scalars = pl.BlockSpec(memory_space=pltpu.SMEM)
    piece = (per_group, depth, rows, width)
    near_k, near_b = math.gcd(kgrp, 2), math.gcd(band, 2)
    wide_k, wide_b = kgrp // near_k, band // near_b
    half = wide_k * per_group
    spread = (slabs, wide_b, near_b, rows, vb)
    return pl.pallas_call(
        functools.partial(fused_kernel, kgrp, band),
        in_specs=[scalars, scalars, scalars, anywhere, anywhere],
        out_specs=[anywhere, pl.BlockSpec(memory_space=pltpu.VMEM)],
        out_shape=[
            jax.ShapeDtypeStruct((chunks, devices) + piece, kind),
            jax.ShapeDtypeStruct((rows, per_group, slabs, vb), kind),
        ],
        scratch_shapes=[
            pltpu.VMEM((per_group * g_all // span, span, rows, width), kind),
            pltpu.VMEM((2, rows, width, span), kind),
            pltpu.VMEM((SLOTS, devices) + piece, kind),
            pltpu.VMEM((devices,) + piece, kind),
            pltpu.VMEM((pairs,) + amplitudes.shape[1:], kind),
            pltpu.VMEM((pairs,) + spread, jnp.float32),
            pltpu.VMEM((max(near_k - 1, 1), half) + spread, kind),
            pltpu.VMEM((max(near_k - 1, 1), half) + spread, kind),
            pltpu.VMEM((half, near_b, slabs, wide_b, rows, vb), kind),
            pltpu.VMEM((per_group, max(wide_k * near_b - 1, 1), slabs, wide_b, rows, vb), kind),
            pltpu.VMEM((per_group, max(wide_b - 1, 1), slabs, rows, vb), kind),
            pltpu.VMEM((per_group, max(wide_b - 1, 1), slabs, rows, vb), kind),
            pltpu.SemaphoreType.DMA((2,)),
            pltpu.SemaphoreType.DMA((SLOTS,)),
            pltpu.SemaphoreType.DMA((chunks,)),
            pltpu.SemaphoreType.DMA,
            pltpu.SemaphoreType.DMA,
            pltpu.SemaphoreType.DMA,
            pltpu.SemaphoreType.DMA,
            pltpu.SemaphoreType.DMA((half,)),
            pltpu.SemaphoreType.DMA,
            pltpu.SemaphoreType.DMA((per_group,)),
            pltpu.SemaphoreType.DMA,
            pltpu.SemaphoreType.DMA((per_group,)),
        ],
        compiler_params=pltpu.CompilerParams(
            collective_id=0, has_side_effects=True, vmem_limit_bytes=62 * 1024 * 1024
        ),
        name="fused",
    )(partner, index, factors, densities, amplitudes)


def shards(kgrp, band, densities, amplitudes, partner, qtable, grid_map, coulomb):
    per_group = densities.shape[0]
    own_ids = lax.axis_index("kgrp") * per_group + jnp.arange(per_group, dtype=jnp.int32)
    transfers = jnp.take(qtable, own_ids)
    index = jnp.take(grid_map, transfers, axis=0)
    factors = jnp.take(coulomb, transfers, axis=0)
    return fused(kgrp, band, densities, amplitudes, partner, index, factors)[1]


def solution(mesh):
    in_specs = (P("kgrp", "band", None, None), P("kgrp", None, None, None), P(), P(), P(), P())
    out_specs = P("band", "kgrp", None, None)
    body = functools.partial(shards, mesh.shape["kgrp"], mesh.shape["band"])
    return jax.shard_map(body, mesh=mesh, in_specs=in_specs, out_specs=out_specs, check_vma=False)
```

```python
import functools
import math

import jax
import jax.numpy as jnp
from jax import lax
from jax.experimental import pallas as pl
from jax.experimental.pallas import tpu as pltpu
from jax.sharding import PartitionSpec as P

MESH = pl.DeviceIdType.MESH
SLOTS = 3
DEPTH = 4
STAGES = 4


def fused_kernel(
    kgrp, band, partner_ref, qtable_ref, densities_ref, amplitudes_ref, grid_ref, coulomb_ref,
    recv_ref, out_ref,
    grids, kernels, index_rows, factor_rows, index_ref, factor_ref,
    turned, staged, slots, block, amps, total,
    core_out, core_in, chip_out, chip_in, far_out, far_in,
    table_sem, turn_sem, send_sem, recv_sem, amp_send, amp_recv, load_sem,
    core_sent, core_came, chip_sent, chip_came, far_sent, far_came,
):
    devices = kgrp * band
    per_group, rows, width, g_all = densities_ref.shape
    split, part_rows = turned.shape[2:4]
    rows_by_g = turned.reshape(per_group * g_all, split, part_rows, width)
    chunks = recv_ref.shape[0]
    depth = slots.shape[3]
    slabs = amps.shape[1]
    g_shard = chunks * depth
    pairs = kgrp * per_group
    vb = band * rows
    my_k, my_b = lax.axis_index("kgrp"), lax.axis_index("band")
    me = my_k * band + my_b
    near_k, near_b = math.gcd(kgrp, 2), math.gcd(band, 2)
    wide_k, wide_b = kgrp // near_k, band // near_b
    my_x, my_c = my_k // near_k, lax.rem(my_k, near_k)
    my_z, my_y = my_b // near_b, lax.rem(my_b, near_b)
    half = wide_k * per_group
    away = (near_k - 1) * half

    def peer(m):
        return lax.rem(my_k + lax.rem(m, kgrp), kgrp), lax.rem(my_b + m // kgrp, band)

    span = staged.shape[-1]
    steps = g_all // span

    def fetch(p, h, i):
        return pltpu.make_async_copy(
            densities_ref.at[
                p,
                pl.ds(h * part_rows, part_rows),
                :,
                pl.ds(pl.multiple_of(i * span, span), span),
            ],
            staged.at[lax.rem(i, STAGES)],
            turn_sem.at[lax.rem(i, STAGES)],
        )

    def fetch_first(p, h):
        for i in range(STAGES - 1):
            fetch(p, h, i).start()

    tables = [
        pltpu.make_async_copy(grid_ref, grids, table_sem.at[0]),
        pltpu.make_async_copy(coulomb_ref, kernels, table_sem.at[1]),
    ]
    for copy in tables:
        copy.start()
    fetch_first(0, 0)

    barrier = pltpu.get_barrier_semaphore()

    def greet(m, carry):
        pl.semaphore_signal(barrier, inc=1, device_id=peer(m), device_id_type=MESH)
        return carry

    lax.fori_loop(1, devices, greet, 0)
    for copy in tables:
        copy.wait()
    for p in range(per_group):
        transfer = qtable_ref[my_k * per_group + p]
        index_rows[p] = grids[transfer]
        factor_rows[p] = kernels[transfer]
    tables = [
        pltpu.make_async_copy(index_rows, index_ref, table_sem.at[0]),
        pltpu.make_async_copy(factor_rows, factor_ref, table_sem.at[1]),
    ]
    for copy in tables:
        copy.start()
    pl.semaphore_wait(barrier, devices - 1)
    for copy in tables:
        copy.wait()

    def turn(p, h):
        def one(i, carry):
            @pl.when(i + STAGES - 1 < steps)
            def _():
                fetch(p, h, i + STAGES - 1).start()

            fetch(p, h, i).wait()
            flat = staged[lax.rem(i, STAGES)].reshape(part_rows * width, span)
            turned[p * steps + i, :, h] = flat.T.reshape(span, part_rows, width)
            return carry

        lax.fori_loop(0, steps, one, 0)

    def pick(p, chunk, *part):
        slot = lax.rem(chunk, SLOTS)

        def one(d, carry):
            first = d * g_shard + chunk * depth
            for j in range(depth):
                source = (p * g_all + index_ref[p, first + j],) + part
                row = rows_by_g[source].astype(jnp.float32) * factor_ref[p, first + j]
                slots[(slot, d, p, j) + part] = row.astype(slots.dtype)
            return carry

        lax.fori_loop(0, devices, one, 0, unroll=2)

    def send(chunk, piece):
        slot = lax.rem(chunk, SLOTS)

        def one(m, carry):
            to_k, to_b = peer(m)
            pltpu.make_async_remote_copy(
                src_ref=piece(slots.at[slot, to_k * band + to_b]),
                dst_ref=piece(recv_ref.at[chunk, me]),
                send_sem=send_sem.at[slot],
                recv_sem=recv_sem.at[chunk],
                device_id=(to_k, to_b),
                device_id_type=MESH,
            ).start()
            return carry

        lax.fori_loop(1, devices, one, 0)
        pltpu.make_async_copy(piece(slots.at[slot, me]), piece(recv_ref.at[chunk, me]), send_sem.at[slot]).start()

    def core_copy(r, step_c, order, to_c):
        at = step_c - 1
        core_out[at, order] = total[r].astype(core_out.dtype)
        pltpu.make_async_remote_copy(
            src_ref=core_out.at[at, order],
            dst_ref=core_in.at[at, order],
            send_sem=core_sent,
            recv_sem=core_came.at[order],
            device_id=(my_x * near_k + to_c, my_b),
            device_id_type=MESH,
        ).start()

    def chip_copies(r, step_x, order, pair, to_x):
        if near_k > 1:
            came = core_in.at[:, order]
            pltpu.make_async_copy(came, came, core_came.at[order]).wait()
        for step_y in range(near_b):
            to_y = lax.rem(my_y + step_y, near_b)
            value = total[r, :, :, to_y]
            for at in range(near_k - 1):
                value = value + core_in[at, order, :, :, to_y].astype(jnp.float32)

            def leave(value=value, step_y=step_y, to_y=to_y):
                chip_out[order, step_y] = value.astype(chip_out.dtype)
                pltpu.make_async_remote_copy(
                    src_ref=chip_out.at[order, step_y],
                    dst_ref=chip_in.at[pair, step_x * near_b + step_y - 1],
                    send_sem=chip_sent,
                    recv_sem=chip_came.at[pair],
                    device_id=(to_x * near_k + my_c, my_z * near_b + to_y),
                    device_id_type=MESH,
                ).start()

            def keep(value=value, to_y=to_y):
                total[r, :, :, to_y] = value

            if step_y:
                leave()
            else:
                pl.when(step_x > 0)(leave)
                pl.when(step_x == 0)(keep)

    def finish():
        own = [my_k * per_group + pair for pair in range(per_group)]
        peers = wide_k * near_b - 1

        def gathered(pair, z):
            value = total[own[pair], :, z, my_y]
            for at in range(peers):
                value = value + chip_in[pair, at, :, z].astype(jnp.float32)
            return value

        for pair in range(per_group):
            if peers:
                pltpu.make_async_copy(chip_in.at[pair], chip_in.at[pair], chip_came.at[pair]).wait()

            def one(step, carry, pair=pair):
                to_z = lax.rem(my_z + step, wide_b)
                far_out[pair, step - 1] = gathered(pair, to_z).astype(far_out.dtype)
                pltpu.make_async_remote_copy(
                    src_ref=far_out.at[pair, step - 1],
                    dst_ref=far_in.at[pair, step - 1],
                    send_sem=far_sent,
                    recv_sem=far_came.at[pair],
                    device_id=(my_k, to_z * near_b + my_y),
                    device_id_type=MESH,
                ).start()
                return carry

            lax.fori_loop(1, wide_b, one, 0)
        for pair in range(per_group):
            value = gathered(pair, my_z)
            if wide_b > 1:
                pltpu.make_async_copy(far_in.at[pair], far_in.at[pair], far_came.at[pair]).wait()
            for at in range(wide_b - 1):
                value = value + far_in[pair, at].astype(jnp.float32)
            value = value * (1.0 / math.sqrt(g_all))
            out_ref[:, pair] = jnp.swapaxes(value, 0, 1).astype(out_ref.dtype)
        if near_k > 1:
            pltpu.make_async_copy(core_out, core_out, core_sent).wait()
        for order in range(half):
            for step_y in range(near_b):
                if step_y or order < half - per_group:
                    sent = chip_out.at[order, step_y]
                    pltpu.make_async_copy(sent, sent, chip_sent).wait()
        if wide_b > 1:
            pltpu.make_async_copy(far_out, far_out, far_sent).wait()

    def ladder(chunk):
        others = pl.ds(0, devices - 1)
        pltpu.make_async_copy(
            recv_ref.at[chunk, others], recv_ref.at[chunk, others], recv_sem.at[chunk]
        ).wait()
        load = pltpu.make_async_copy(recv_ref.at[chunk], block, load_sem)
        load.start()
        load.wait()

        def one(i, carry):
            order = lax.rem(i, half)
            step_c, step_x, pair = near_k - 1 - i // half, wide_k - 1 - order // per_group, lax.rem(order, per_group)
            to_c, to_x = lax.rem(my_c + step_c, near_k), lax.rem(my_x + step_x, wide_k)
            r = (to_x * near_k + to_c) * per_group + pair
            q = partner_ref[r]
            left_base, left_pair = r // per_group * band, lax.rem(r, per_group)
            right_base, right_pair = q // per_group * band, lax.rem(q, per_group)
            left = jnp.concatenate(
                [block[left_base + b, left_pair, j].reshape(rows, width) for j in range(depth) for b in range(band)], axis=0
            )
            right = jnp.concatenate(
                [
                    jnp.concatenate(
                        [block[right_base + b, right_pair, j].reshape(rows, width) for b in range(band)], axis=0
                    )
                    for j in range(depth)
                ],
                axis=1,
            )
            amp = jnp.concatenate([amps[r, s] for s in range(slabs)], axis=1)
            mixed = jnp.dot(left, amp, preferred_element_type=jnp.float32).astype(jnp.bfloat16)
            wide = jnp.concatenate(
                [
                    jnp.concatenate(
                        [mixed[j * vb:(j + 1) * vb, s * width:(s + 1) * width] for j in range(depth)], axis=1
                    )
                    for s in range(slabs)
                ],
                axis=0,
            )
            part = lax.dot_general(wide, right, (((1,), (1,)), ((), ())), preferred_element_type=jnp.float32)
            total[r] += part.reshape(slabs, wide_b, near_b, rows, vb)

            @pl.when((chunk == chunks - 1) & (i < away))
            def _():
                core_copy(r, step_c, order, to_c)

            @pl.when((chunk == chunks - 1) & (i >= away))
            def _():
                chip_copies(r, step_x, order, pair, to_x)

            return carry

        lax.fori_loop(0, pairs, one, 0)

    def amp_copy(m):
        to_k = lax.rem(my_k + m, kgrp)
        return pltpu.make_async_remote_copy(
            src_ref=amplitudes_ref,
            dst_ref=amps.at[pl.ds(my_k * per_group, per_group)],
            send_sem=amp_send,
            recv_sem=amp_recv,
            device_id=(to_k, my_b),
            device_id_type=MESH,
        )

    own_amp = pltpu.make_async_copy(amplitudes_ref, amps.at[pl.ds(my_k * per_group, per_group)], load_sem)

    def begin(p, carry):
        for h in range(split):
            turn(p, h)
            if h + 1 < split:
                fetch_first(p, h + 1)
            else:
                pl.when(p + 1 < per_group)(functools.partial(fetch_first, p + 1, 0))
            for chunk in range(SLOTS):
                pick(p, chunk, h)
                if chunk:
                    send(chunk - 1, lambda ref: ref.at[p, :, h])
            send(SLOTS - 1, lambda ref: ref.at[p, :, h])
        return carry

    total[...] = jnp.zeros_like(total)
    lax.fori_loop(0, per_group, begin, 0)
    own_amp.start()
    for m in range(1, kgrp):
        amp_copy(m).start()
    own_amp.wait()
    all_amps = amps.at[pl.ds(0, (kgrp - 1) * per_group)]
    pltpu.make_async_copy(all_amps, all_amps, amp_send).wait()
    pltpu.make_async_copy(all_amps, all_amps, amp_recv).wait()

    def main(chunk, carry):
        slot = lax.rem(chunk, SLOTS)
        pltpu.make_async_copy(slots.at[slot], slots.at[slot], send_sem.at[slot]).wait()

        @pl.when(chunk < chunks)
        def _():
            for p in range(per_group):
                pick(p, chunk)

        ladder(chunk - SLOTS)

        @pl.when(chunk < chunks)
        def _():
            send(chunk, lambda ref: ref)

        return carry

    lax.fori_loop(SLOTS, chunks + SLOTS, main, 0)
    finish()


def fused(kgrp, band, densities, amplitudes, partner, qtable, grid_map, coulomb):
    per_group, rows, width, g_all = densities.shape
    slabs = amplitudes.shape[1]
    devices = kgrp * band
    pairs = kgrp * per_group
    vb = rows * band
    g_shard = g_all // devices
    depth = math.gcd(g_shard, DEPTH)
    chunks = g_shard // depth
    span = math.gcd(g_all, 256)
    kind = densities.dtype
    anywhere = pl.BlockSpec(memory_space=pl.ANY)
    scalars = pl.BlockSpec(memory_space=pltpu.SMEM)
    split = math.gcd(max(rows // 8, 1), 2)
    part_rows = rows // split
    piece = (per_group, depth, split, part_rows, width)
    near_k, near_b = math.gcd(kgrp, 2), math.gcd(band, 2)
    wide_k, wide_b = kgrp // near_k, band // near_b
    half = wide_k * per_group
    spread = (slabs, wide_b, near_b, rows, vb)
    return pl.pallas_call(
        functools.partial(fused_kernel, kgrp, band),
        in_specs=[scalars, scalars, anywhere, anywhere, anywhere, anywhere],
        out_specs=[anywhere, pl.BlockSpec(memory_space=pltpu.VMEM)],
        out_shape=[
            jax.ShapeDtypeStruct((chunks, devices) + piece, kind),
            jax.ShapeDtypeStruct((rows, per_group, slabs, vb), kind),
        ],
        scratch_shapes=[
            pltpu.VMEM(grid_map.shape, grid_map.dtype),
            pltpu.VMEM(coulomb.shape, coulomb.dtype),
            pltpu.VMEM((per_group, g_all), grid_map.dtype),
            pltpu.VMEM((per_group, g_all), coulomb.dtype),
            pltpu.SMEM((per_group, g_all), grid_map.dtype),
            pltpu.SMEM((per_group, g_all), coulomb.dtype),
            pltpu.VMEM((per_group * g_all // span, span, split, part_rows, width), kind),
            pltpu.VMEM((STAGES, part_rows, width, span), kind),
            pltpu.VMEM((SLOTS, devices) + piece, kind),
            pltpu.VMEM((devices,) + piece, kind),
            pltpu.VMEM((pairs,) + amplitudes.shape[1:], kind),
            pltpu.VMEM((pairs,) + spread, jnp.float32),
            pltpu.VMEM((max(near_k - 1, 1), half) + spread, kind),
            pltpu.VMEM((max(near_k - 1, 1), half) + spread, kind),
            pltpu.VMEM((half, near_b, slabs, wide_b, rows, vb), kind),
            pltpu.VMEM((per_group, max(wide_k * near_b - 1, 1), slabs, wide_b, rows, vb), kind),
            pltpu.VMEM((per_group, max(wide_b - 1, 1), slabs, rows, vb), kind),
            pltpu.VMEM((per_group, max(wide_b - 1, 1), slabs, rows, vb), kind),
            pltpu.SemaphoreType.DMA((2,)),
            pltpu.SemaphoreType.DMA((STAGES,)),
            pltpu.SemaphoreType.DMA((SLOTS,)),
            pltpu.SemaphoreType.DMA((chunks,)),
            pltpu.SemaphoreType.DMA,
            pltpu.SemaphoreType.DMA,
            pltpu.SemaphoreType.DMA,
            pltpu.SemaphoreType.DMA,
            pltpu.SemaphoreType.DMA((half,)),
            pltpu.SemaphoreType.DMA,
            pltpu.SemaphoreType.DMA((per_group,)),
            pltpu.SemaphoreType.DMA,
            pltpu.SemaphoreType.DMA((per_group,)),
        ],
        compiler_params=pltpu.CompilerParams(
            collective_id=0, has_side_effects=True, vmem_limit_bytes=62 * 1024 * 1024
        ),
        name="fused",
    )(partner, qtable, densities, amplitudes, grid_map, coulomb)


def shards(kgrp, band, densities, amplitudes, partner, qtable, grid_map, coulomb):
    return fused(kgrp, band, densities, amplitudes, partner, qtable, grid_map, coulomb)[1]


def solution(mesh):
    in_specs = (P("kgrp", "band", None, None), P("kgrp", None, None, None), P(), P(), P(), P())
    out_specs = P("band", "kgrp", None, None)
    body = functools.partial(shards, mesh.shape["kgrp"], mesh.shape["band"])
    return jax.shard_map(body, mesh=mesh, in_specs=in_specs, out_specs=out_specs, check_vma=False)
```

```python
import functools
import math

import jax
import jax.numpy as jnp
from jax import lax
from jax.experimental import pallas as pl
from jax.experimental.pallas import tpu as pltpu
from jax.sharding import PartitionSpec as P

MESH = pl.DeviceIdType.MESH
SLOTS = 6
DEPTH = 4
STAGES = 4
LAG = 2


def fused_kernel(
    kgrp, band, partner_ref, qtable_ref, densities_ref, amplitudes_ref, grid_ref, coulomb_ref,
    recv_ref, out_ref,
    grids, kernels, index_rows, factor_rows, index_ref, factor_ref,
    turned, staged, slots, block, amps, total,
    core_out, core_in, chip_out, chip_in, far_out, far_in,
    table_sem, turn_sem, send_sem, recv_sem, amp_send, amp_recv, load_sem,
    core_sent, core_came, chip_sent, chip_came, far_sent, far_came,
):
    devices = kgrp * band
    per_group, rows, width, g_all = densities_ref.shape
    split, part_rows = turned.shape[2:4]
    rows_by_g = turned.reshape(per_group * g_all, split, part_rows, width)
    chunks = recv_ref.shape[0]
    ahead, depth = slots.shape[0], slots.shape[3]
    slabs = amps.shape[1]
    g_shard = chunks * depth
    pairs = kgrp * per_group
    vb = band * rows
    my_k, my_b = lax.axis_index("kgrp"), lax.axis_index("band")
    me = my_k * band + my_b
    near_k, near_b = math.gcd(kgrp, 2), math.gcd(band, 2)
    wide_k, wide_b = kgrp // near_k, band // near_b
    my_x, my_c = my_k // near_k, lax.rem(my_k, near_k)
    my_z, my_y = my_b // near_b, lax.rem(my_b, near_b)
    half = wide_k * per_group
    away = (near_k - 1) * half

    def peer(m):
        return lax.rem(my_k + lax.rem(m, kgrp), kgrp), lax.rem(my_b + m // kgrp, band)

    span = staged.shape[-1]
    steps = g_all // span

    def fetch(p, h, i):
        return pltpu.make_async_copy(
            densities_ref.at[
                p,
                pl.ds(h * part_rows, part_rows),
                :,
                pl.ds(pl.multiple_of(i * span, span), span),
            ],
            staged.at[lax.rem(i, STAGES)],
            turn_sem.at[lax.rem(i, STAGES)],
        )

    def fetch_first(p, h):
        for i in range(STAGES - 1):
            fetch(p, h, i).start()

    tables = [
        pltpu.make_async_copy(grid_ref, grids, table_sem.at[0]),
        pltpu.make_async_copy(coulomb_ref, kernels, table_sem.at[1]),
    ]
    for copy in tables:
        copy.start()
    fetch_first(0, 0)

    barrier = pltpu.get_barrier_semaphore()

    def greet(m, carry):
        pl.semaphore_signal(barrier, inc=1, device_id=peer(m), device_id_type=MESH)
        return carry

    lax.fori_loop(1, devices, greet, 0)
    for copy in tables:
        copy.wait()
    for p in range(per_group):
        transfer = qtable_ref[my_k * per_group + p]
        index_rows[p] = grids[transfer]
        factor_rows[p] = kernels[transfer]
    tables = [
        pltpu.make_async_copy(index_rows, index_ref, table_sem.at[0]),
        pltpu.make_async_copy(factor_rows, factor_ref, table_sem.at[1]),
    ]
    for copy in tables:
        copy.start()
    pl.semaphore_wait(barrier, devices - 1)
    for copy in tables:
        copy.wait()

    def turn(p, h):
        def one(i, carry):
            @pl.when(i + STAGES - 1 < steps)
            def _():
                fetch(p, h, i + STAGES - 1).start()

            fetch(p, h, i).wait()
            flat = staged[lax.rem(i, STAGES)].reshape(part_rows * width, span)
            turned[p * steps + i, :, h] = flat.T.reshape(span, part_rows, width)
            return carry

        lax.fori_loop(0, steps, one, 0)

    def pick(p, chunk, d, *part):
        slot, first = lax.rem(chunk, ahead), d * g_shard + chunk * depth
        for j in range(depth):
            source = (p * g_all + index_ref[p, first + j],) + part
            row = rows_by_g[source].astype(jnp.float32) * factor_ref[p, first + j]
            slots[(slot, d, p, j) + part] = row.astype(slots.dtype)

    def pick_all(p, chunk):
        def one(d, carry):
            pick(p, chunk, d)
            return carry

        lax.fori_loop(0, devices, one, 0, unroll=2)

    def send(chunk, m, piece):
        slot = lax.rem(chunk, ahead)
        to_k, to_b = peer(m)
        pltpu.make_async_remote_copy(
            src_ref=piece(slots.at[slot, to_k * band + to_b]),
            dst_ref=piece(recv_ref.at[chunk, me]),
            send_sem=send_sem.at[slot],
            recv_sem=recv_sem.at[chunk],
            device_id=(to_k, to_b),
            device_id_type=MESH,
        ).start()

    def put(chunk, piece):
        slot = lax.rem(chunk, ahead)
        pltpu.make_async_copy(piece(slots.at[slot, me]), piece(recv_ref.at[chunk, me]), send_sem.at[slot]).start()

    def send_all(chunk):
        def one(m, carry):
            send(chunk, m, lambda ref: ref)
            return carry

        lax.fori_loop(1, devices, one, 0)
        put(chunk, lambda ref: ref)

    def pick_and_send(p, h, chunk):
        def piece(ref):
            return ref.at[p, :, h]

        def turned_to(i):
            return lax.rem(i + devices // 2, devices)

        def one(i, carry):
            @pl.when(i < devices)
            def _():
                to_k, to_b = peer(turned_to(i))
                pick(p, chunk, to_k * band + to_b, h)

            m = turned_to(i + devices - LAG)

            @pl.when((i >= LAG) & (m > 0))
            def _():
                send(chunk, m, piece)

            return carry

        lax.fori_loop(0, devices + LAG, one, 0)
        put(chunk, piece)

    def core_copy(r, step_c, order, to_c):
        at = step_c - 1
        core_out[at, order] = total[r].astype(core_out.dtype)
        pltpu.make_async_remote_copy(
            src_ref=core_out.at[at, order],
            dst_ref=core_in.at[at, order],
            send_sem=core_sent,
            recv_sem=core_came.at[order],
            device_id=(my_x * near_k + to_c, my_b),
            device_id_type=MESH,
        ).start()

    def chip_copies(r, step_x, order, pair, to_x):
        if near_k > 1:
            came = core_in.at[:, order]
            pltpu.make_async_copy(came, came, core_came.at[order]).wait()
        for step_y in range(near_b):
            to_y = lax.rem(my_y + step_y, near_b)
            value = total[r, :, :, to_y]
            for at in range(near_k - 1):
                value = value + core_in[at, order, :, :, to_y].astype(jnp.float32)

            def leave(value=value, step_y=step_y, to_y=to_y):
                chip_out[order, step_y] = value.astype(chip_out.dtype)
                pltpu.make_async_remote_copy(
                    src_ref=chip_out.at[order, step_y],
                    dst_ref=chip_in.at[pair, step_x * near_b + step_y - 1],
                    send_sem=chip_sent,
                    recv_sem=chip_came.at[pair],
                    device_id=(to_x * near_k + my_c, my_z * near_b + to_y),
                    device_id_type=MESH,
                ).start()

            def keep(value=value, to_y=to_y):
                total[r, :, :, to_y] = value

            if step_y:
                leave()
            else:
                pl.when(step_x > 0)(leave)
                pl.when(step_x == 0)(keep)

    def finish():
        own = [my_k * per_group + pair for pair in range(per_group)]
        peers = wide_k * near_b - 1

        def gathered(pair, z):
            value = total[own[pair], :, z, my_y]
            for at in range(peers):
                value = value + chip_in[pair, at, :, z].astype(jnp.float32)
            return value

        for pair in range(per_group):
            if peers:
                pltpu.make_async_copy(chip_in.at[pair], chip_in.at[pair], chip_came.at[pair]).wait()

            def one(step, carry, pair=pair):
                to_z = lax.rem(my_z + step, wide_b)
                far_out[pair, step - 1] = gathered(pair, to_z).astype(far_out.dtype)
                pltpu.make_async_remote_copy(
                    src_ref=far_out.at[pair, step - 1],
                    dst_ref=far_in.at[pair, step - 1],
                    send_sem=far_sent,
                    recv_sem=far_came.at[pair],
                    device_id=(my_k, to_z * near_b + my_y),
                    device_id_type=MESH,
                ).start()
                return carry

            lax.fori_loop(1, wide_b, one, 0)
        for pair in range(per_group):
            value = gathered(pair, my_z)
            if wide_b > 1:
                pltpu.make_async_copy(far_in.at[pair], far_in.at[pair], far_came.at[pair]).wait()
            for at in range(wide_b - 1):
                value = value + far_in[pair, at].astype(jnp.float32)
            value = value * (1.0 / math.sqrt(g_all))
            out_ref[:, pair] = jnp.swapaxes(value, 0, 1).astype(out_ref.dtype)
        if near_k > 1:
            pltpu.make_async_copy(core_out, core_out, core_sent).wait()
        for order in range(half):
            for step_y in range(near_b):
                if step_y or order < half - per_group:
                    sent = chip_out.at[order, step_y]
                    pltpu.make_async_copy(sent, sent, chip_sent).wait()
        if wide_b > 1:
            pltpu.make_async_copy(far_out, far_out, far_sent).wait()

    def ladder(chunk):
        others = pl.ds(0, devices - 1)
        pltpu.make_async_copy(
            recv_ref.at[chunk, others], recv_ref.at[chunk, others], recv_sem.at[chunk]
        ).wait()
        load = pltpu.make_async_copy(recv_ref.at[chunk], block, load_sem)
        load.start()
        load.wait()

        def one(i, carry):
            order = lax.rem(i, half)
            step_c, step_x, pair = near_k - 1 - i // half, wide_k - 1 - order // per_group, lax.rem(order, per_group)
            to_c, to_x = lax.rem(my_c + step_c, near_k), lax.rem(my_x + step_x, wide_k)
            r = (to_x * near_k + to_c) * per_group + pair
            q = partner_ref[r]
            left_base, left_pair = r // per_group * band, lax.rem(r, per_group)
            right_base, right_pair = q // per_group * band, lax.rem(q, per_group)
            left = jnp.concatenate(
                [block[left_base + b, left_pair, j].reshape(rows, width) for j in range(depth) for b in range(band)], axis=0
            )
            right = jnp.concatenate(
                [
                    jnp.concatenate(
                        [block[right_base + b, right_pair, j].reshape(rows, width) for b in range(band)], axis=0
                    )
                    for j in range(depth)
                ],
                axis=1,
            )
            amp = jnp.concatenate([amps[r, s] for s in range(slabs)], axis=1)
            mixed = jnp.dot(left, amp, preferred_element_type=jnp.float32).astype(jnp.bfloat16)
            wide = jnp.concatenate(
                [
                    jnp.concatenate(
                        [mixed[j * vb:(j + 1) * vb, s * width:(s + 1) * width] for j in range(depth)], axis=1
                    )
                    for s in range(slabs)
                ],
                axis=0,
            )
            part = lax.dot_general(wide, right, (((1,), (1,)), ((), ())), preferred_element_type=jnp.float32)
            total[r] += part.reshape(slabs, wide_b, near_b, rows, vb)

            @pl.when((chunk == chunks - 1) & (i < away))
            def _():
                core_copy(r, step_c, order, to_c)

            @pl.when((chunk == chunks - 1) & (i >= away))
            def _():
                chip_copies(r, step_x, order, pair, to_x)

            return carry

        lax.fori_loop(0, pairs, one, 0)

    def amp_copy(m):
        to_k = lax.rem(my_k + m, kgrp)
        return pltpu.make_async_remote_copy(
            src_ref=amplitudes_ref,
            dst_ref=amps.at[pl.ds(my_k * per_group, per_group)],
            send_sem=amp_send,
            recv_sem=amp_recv,
            device_id=(to_k, my_b),
            device_id_type=MESH,
        )

    own_amp = pltpu.make_async_copy(amplitudes_ref, amps.at[pl.ds(my_k * per_group, per_group)], load_sem)

    def begin(p, carry):
        for h in range(split):
            turn(p, h)
            if h + 1 < split:
                fetch_first(p, h + 1)
            else:
                pl.when(p + 1 < per_group)(functools.partial(fetch_first, p + 1, 0))

            def one(chunk, inner, h=h):
                pick_and_send(p, h, chunk)
                return inner

            lax.fori_loop(0, ahead, one, 0)
        return carry

    total[...] = jnp.zeros_like(total)
    lax.fori_loop(0, per_group, begin, 0)
    own_amp.start()
    for m in range(1, kgrp):
        amp_copy(m).start()
    own_amp.wait()
    all_amps = amps.at[pl.ds(0, (kgrp - 1) * per_group)]
    pltpu.make_async_copy(all_amps, all_amps, amp_send).wait()
    pltpu.make_async_copy(all_amps, all_amps, amp_recv).wait()

    def main(chunk, carry):
        slot = lax.rem(chunk, ahead)
        pltpu.make_async_copy(slots.at[slot], slots.at[slot], send_sem.at[slot]).wait()

        @pl.when(chunk < chunks)
        def _():
            for p in range(per_group):
                pick_all(p, chunk)

        ladder(chunk - ahead)

        @pl.when(chunk < chunks)
        def _():
            send_all(chunk)

        return carry

    lax.fori_loop(ahead, chunks + ahead, main, 0)
    finish()


def fused(kgrp, band, densities, amplitudes, partner, qtable, grid_map, coulomb):
    per_group, rows, width, g_all = densities.shape
    slabs = amplitudes.shape[1]
    devices = kgrp * band
    pairs = kgrp * per_group
    vb = rows * band
    g_shard = g_all // devices
    depth = math.gcd(g_shard, DEPTH)
    chunks = g_shard // depth
    ahead = min(SLOTS, chunks)
    span = math.gcd(g_all, 256)
    kind = densities.dtype
    anywhere = pl.BlockSpec(memory_space=pl.ANY)
    scalars = pl.BlockSpec(memory_space=pltpu.SMEM)
    split = math.gcd(max(rows // 8, 1), 2)
    part_rows = rows // split
    piece = (per_group, depth, split, part_rows, width)
    near_k, near_b = math.gcd(kgrp, 2), math.gcd(band, 2)
    wide_k, wide_b = kgrp // near_k, band // near_b
    half = wide_k * per_group
    spread = (slabs, wide_b, near_b, rows, vb)
    return pl.pallas_call(
        functools.partial(fused_kernel, kgrp, band),
        in_specs=[scalars, scalars, anywhere, anywhere, anywhere, anywhere],
        out_specs=[anywhere, pl.BlockSpec(memory_space=pltpu.VMEM)],
        out_shape=[
            jax.ShapeDtypeStruct((chunks, devices) + piece, kind),
            jax.ShapeDtypeStruct((rows, per_group, slabs, vb), kind),
        ],
        scratch_shapes=[
            pltpu.VMEM(grid_map.shape, grid_map.dtype),
            pltpu.VMEM(coulomb.shape, coulomb.dtype),
            pltpu.VMEM((per_group, g_all), grid_map.dtype),
            pltpu.VMEM((per_group, g_all), coulomb.dtype),
            pltpu.SMEM((per_group, g_all), grid_map.dtype),
            pltpu.SMEM((per_group, g_all), coulomb.dtype),
            pltpu.VMEM((per_group * g_all // span, span, split, part_rows, width), kind),
            pltpu.VMEM((STAGES, part_rows, width, span), kind),
            pltpu.VMEM((ahead, devices) + piece, kind),
            pltpu.VMEM((devices,) + piece, kind),
            pltpu.VMEM((pairs,) + amplitudes.shape[1:], kind),
            pltpu.VMEM((pairs,) + spread, jnp.float32),
            pltpu.VMEM((max(near_k - 1, 1), half) + spread, kind),
            pltpu.VMEM((max(near_k - 1, 1), half) + spread, kind),
            pltpu.VMEM((half, near_b, slabs, wide_b, rows, vb), kind),
            pltpu.VMEM((per_group, max(wide_k * near_b - 1, 1), slabs, wide_b, rows, vb), kind),
            pltpu.VMEM((per_group, max(wide_b - 1, 1), slabs, rows, vb), kind),
            pltpu.VMEM((per_group, max(wide_b - 1, 1), slabs, rows, vb), kind),
            pltpu.SemaphoreType.DMA((2,)),
            pltpu.SemaphoreType.DMA((STAGES,)),
            pltpu.SemaphoreType.DMA((ahead,)),
            pltpu.SemaphoreType.DMA((chunks,)),
            pltpu.SemaphoreType.DMA,
            pltpu.SemaphoreType.DMA,
            pltpu.SemaphoreType.DMA,
            pltpu.SemaphoreType.DMA,
            pltpu.SemaphoreType.DMA((half,)),
            pltpu.SemaphoreType.DMA,
            pltpu.SemaphoreType.DMA((per_group,)),
            pltpu.SemaphoreType.DMA,
            pltpu.SemaphoreType.DMA((per_group,)),
        ],
        compiler_params=pltpu.CompilerParams(
            collective_id=0, has_side_effects=True, vmem_limit_bytes=63 * 1024 * 1024
        ),
        name="fused",
    )(partner, qtable, densities, amplitudes, grid_map, coulomb)


def shards(kgrp, band, densities, amplitudes, partner, qtable, grid_map, coulomb):
    return fused(kgrp, band, densities, amplitudes, partner, qtable, grid_map, coulomb)[1]


def solution(mesh):
    in_specs = (P("kgrp", "band", None, None), P("kgrp", None, None, None), P(), P(), P(), P())
    out_specs = P("band", "kgrp", None, None)
    body = functools.partial(shards, mesh.shape["kgrp"], mesh.shape["band"])
    return jax.shard_map(body, mesh=mesh, in_specs=in_specs, out_specs=out_specs, check_vma=False)
```

```python
import functools
import math

import jax
import jax.numpy as jnp
from jax import lax
from jax.experimental import pallas as pl
from jax.experimental.pallas import tpu as pltpu
from jax.sharding import PartitionSpec as P

MESH = pl.DeviceIdType.MESH
SLOTS = 7
DEPTH = 4
STAGES = 4
LAG = 2


def fused_kernel(
    kgrp, band, partner_ref, qtable_ref, densities_ref, amplitudes_ref, grid_ref, coulomb_ref,
    recv_ref, out_ref,
    grids, kernels, index_rows, factor_rows, index_ref, factor_ref,
    turned, staged, slots, block, amps, total,
    core_out, core_in, chip_out, chip_in, far_out, far_in,
    table_sem, turn_sem, send_sem, recv_sem, amp_send, amp_recv, load_sem,
    core_sent, core_came, chip_sent, chip_came, far_sent, far_came,
):
    devices = kgrp * band
    per_group, rows, width, g_all = densities_ref.shape
    split, part_rows = turned.shape[2:4]
    rows_by_g = turned.reshape(per_group * g_all, split, part_rows, width)
    chunks = recv_ref.shape[0]
    ahead, depth = slots.shape[0], slots.shape[3]
    slabs = amps.shape[1]
    g_shard = chunks * depth
    pairs = kgrp * per_group
    vb = band * rows
    my_k, my_b = lax.axis_index("kgrp"), lax.axis_index("band")
    me = my_k * band + my_b
    near_k, near_b = math.gcd(kgrp, 2), math.gcd(band, 2)
    wide_k, wide_b = kgrp // near_k, band // near_b
    my_x, my_c = my_k // near_k, lax.rem(my_k, near_k)
    my_z, my_y = my_b // near_b, lax.rem(my_b, near_b)
    half = wide_k * per_group
    away = (near_k - 1) * half

    def peer(m):
        return lax.rem(my_k + lax.rem(m, kgrp), kgrp), lax.rem(my_b + m // kgrp, band)

    span = staged.shape[-1]
    steps = g_all // span

    def fetch(p, h, i):
        return pltpu.make_async_copy(
            densities_ref.at[
                p,
                pl.ds(h * part_rows, part_rows),
                :,
                pl.ds(pl.multiple_of(i * span, span), span),
            ],
            staged.at[lax.rem(i, STAGES)],
            turn_sem.at[lax.rem(i, STAGES)],
        )

    def fetch_first(p, h):
        for i in range(STAGES - 1):
            fetch(p, h, i).start()

    tables = [
        pltpu.make_async_copy(grid_ref, grids, table_sem.at[0]),
        pltpu.make_async_copy(coulomb_ref, kernels, table_sem.at[1]),
    ]
    for copy in tables:
        copy.start()
    fetch_first(0, 0)

    barrier = pltpu.get_barrier_semaphore()

    def greet(m, carry):
        pl.semaphore_signal(barrier, inc=1, device_id=peer(m), device_id_type=MESH)
        return carry

    lax.fori_loop(1, devices, greet, 0)
    for copy in tables:
        copy.wait()
    for p in range(per_group):
        transfer = qtable_ref[my_k * per_group + p]
        index_rows[p] = grids[transfer]
        factor_rows[p] = kernels[transfer]
    tables = [
        pltpu.make_async_copy(index_rows, index_ref, table_sem.at[0]),
        pltpu.make_async_copy(factor_rows, factor_ref, table_sem.at[1]),
    ]
    for copy in tables:
        copy.start()

    def turn(p, h):
        def one(i, carry):
            @pl.when(i + STAGES - 1 < steps)
            def _():
                fetch(p, h, i + STAGES - 1).start()

            fetch(p, h, i).wait()
            flat = staged[lax.rem(i, STAGES)].reshape(part_rows * width, span)
            turned[p * steps + i, :, h] = flat.T.reshape(span, part_rows, width)
            return carry

        lax.fori_loop(0, steps, one, 0)

    def pick(p, chunk, d, *part):
        slot, first = lax.rem(chunk, ahead), d * g_shard + chunk * depth
        for j in range(depth):
            source = (p * g_all + index_ref[p, first + j],) + part
            row = rows_by_g[source].astype(jnp.float32) * factor_ref[p, first + j]
            slots[(slot, d, p, j) + part] = row.astype(slots.dtype)

    def pick_all(p, chunk):
        def one(d, carry):
            pick(p, chunk, d)
            return carry

        lax.fori_loop(0, devices, one, 0, unroll=2)

    def send(chunk, m, piece, came=None):
        slot = lax.rem(chunk, ahead)
        to_k, to_b = peer(m)
        pltpu.make_async_remote_copy(
            src_ref=piece(slots.at[slot, to_k * band + to_b]),
            dst_ref=piece(recv_ref.at[chunk, me]),
            send_sem=send_sem.at[slot],
            recv_sem=recv_sem.at[chunk if came is None else came],
            device_id=(to_k, to_b),
            device_id_type=MESH,
        ).start()

    def put(chunk, piece):
        slot = lax.rem(chunk, ahead)
        pltpu.make_async_copy(piece(slots.at[slot, me]), piece(recv_ref.at[chunk, me]), send_sem.at[slot]).start()

    def send_all(chunk, piece, came=None):
        def one(m, carry):
            send(chunk, m, piece, came)
            return carry

        lax.fori_loop(1, devices, one, 0)
        put(chunk, piece)

    def head_of(ref):
        return ref.at[:, pl.ds(0, depth - 1)]

    def tail_of(ref):
        return ref.at[:, pl.ds(depth - 1, 1)]

    def pick_and_send(p, h, chunk):
        def piece(ref):
            return ref.at[p, :, h]

        def turned_to(i):
            return lax.rem(i + devices // 2, devices)

        def one(i, carry):
            @pl.when(i < devices)
            def _():
                to_k, to_b = peer(turned_to(i))
                pick(p, chunk, to_k * band + to_b, h)

            m = turned_to(i + devices - LAG)

            @pl.when((i >= LAG) & (m > 0))
            def _():
                send(chunk, m, piece)

            return carry

        lax.fori_loop(0, devices + LAG, one, 0)
        put(chunk, piece)

    def core_copy(r, step_c, order, to_c):
        at = step_c - 1
        core_out[at, order] = total[r].astype(core_out.dtype)
        pltpu.make_async_remote_copy(
            src_ref=core_out.at[at, order],
            dst_ref=core_in.at[at, order],
            send_sem=core_sent,
            recv_sem=core_came.at[order],
            device_id=(my_x * near_k + to_c, my_b),
            device_id_type=MESH,
        ).start()

    def chip_copies(r, step_x, order, pair, to_x):
        if near_k > 1:
            came = core_in.at[:, order]
            pltpu.make_async_copy(came, came, core_came.at[order]).wait()
        for step_y in range(near_b):
            to_y = lax.rem(my_y + step_y, near_b)
            value = total[r, :, :, to_y]
            for at in range(near_k - 1):
                value = value + core_in[at, order, :, :, to_y].astype(jnp.float32)

            def leave(value=value, step_y=step_y, to_y=to_y):
                chip_out[order, step_y] = value.astype(chip_out.dtype)
                pltpu.make_async_remote_copy(
                    src_ref=chip_out.at[order, step_y],
                    dst_ref=chip_in.at[pair, step_x * near_b + step_y - 1],
                    send_sem=chip_sent,
                    recv_sem=chip_came.at[pair],
                    device_id=(to_x * near_k + my_c, my_z * near_b + to_y),
                    device_id_type=MESH,
                ).start()

            def keep(value=value, to_y=to_y):
                total[r, :, :, to_y] = value

            if step_y:
                leave()
            else:
                pl.when(step_x > 0)(leave)
                pl.when(step_x == 0)(keep)

    def finish():
        own = [my_k * per_group + pair for pair in range(per_group)]
        peers = wide_k * near_b - 1

        def gathered(pair, z):
            value = total[own[pair], :, z, my_y]
            for at in range(peers):
                value = value + chip_in[pair, at, :, z].astype(jnp.float32)
            return value

        for pair in range(per_group):
            if peers:
                pltpu.make_async_copy(chip_in.at[pair], chip_in.at[pair], chip_came.at[pair]).wait()

            def one(step, carry, pair=pair):
                to_z = lax.rem(my_z + step, wide_b)
                far_out[pair, step - 1] = gathered(pair, to_z).astype(far_out.dtype)
                pltpu.make_async_remote_copy(
                    src_ref=far_out.at[pair, step - 1],
                    dst_ref=far_in.at[pair, step - 1],
                    send_sem=far_sent,
                    recv_sem=far_came.at[pair],
                    device_id=(my_k, to_z * near_b + my_y),
                    device_id_type=MESH,
                ).start()
                return carry

            lax.fori_loop(1, wide_b, one, 0)
        for pair in range(per_group):
            value = gathered(pair, my_z)
            if wide_b > 1:
                pltpu.make_async_copy(far_in.at[pair], far_in.at[pair], far_came.at[pair]).wait()
            for at in range(wide_b - 1):
                value = value + far_in[pair, at].astype(jnp.float32)
            value = value * (1.0 / math.sqrt(g_all))
            out_ref[:, pair] = jnp.swapaxes(value, 0, 1).astype(out_ref.dtype)
        if near_k > 1:
            pltpu.make_async_copy(core_out, core_out, core_sent).wait()
        for order in range(half):
            for step_y in range(near_b):
                if step_y or order < half - per_group:
                    sent = chip_out.at[order, step_y]
                    pltpu.make_async_copy(sent, sent, chip_sent).wait()
        if wide_b > 1:
            pltpu.make_async_copy(far_out, far_out, far_sent).wait()

    def ladder(chunk, first=0, count=depth, came=None, last=False):
        window = (slice(None), slice(None), pl.ds(first, count))
        others = recv_ref.at[(chunk, pl.ds(0, devices - 1)) + window[1:]]
        pltpu.make_async_copy(others, others, recv_sem.at[chunk if came is None else came]).wait()
        load = pltpu.make_async_copy(recv_ref.at[(chunk,) + window], block.at[window], load_sem)
        load.start()
        load.wait()

        def one(i, carry):
            order = lax.rem(i, half)
            step_c, step_x, pair = near_k - 1 - i // half, wide_k - 1 - order // per_group, lax.rem(order, per_group)
            to_c, to_x = lax.rem(my_c + step_c, near_k), lax.rem(my_x + step_x, wide_k)
            r = (to_x * near_k + to_c) * per_group + pair
            q = partner_ref[r]
            left_base, left_pair = r // per_group * band, lax.rem(r, per_group)
            right_base, right_pair = q // per_group * band, lax.rem(q, per_group)
            left = jnp.concatenate(
                [block[left_base + b, left_pair, j].reshape(rows, width) for j in range(first, first + count) for b in range(band)], axis=0
            )
            right = jnp.concatenate(
                [
                    jnp.concatenate(
                        [block[right_base + b, right_pair, j].reshape(rows, width) for b in range(band)], axis=0
                    )
                    for j in range(first, first + count)
                ],
                axis=1,
            )
            amp = jnp.concatenate([amps[r, s] for s in range(slabs)], axis=1)
            mixed = jnp.dot(left, amp, preferred_element_type=jnp.float32).astype(jnp.bfloat16)
            wide = jnp.concatenate(
                [
                    jnp.concatenate(
                        [mixed[j * vb:(j + 1) * vb, s * width:(s + 1) * width] for j in range(count)], axis=1
                    )
                    for s in range(slabs)
                ],
                axis=0,
            )
            part = lax.dot_general(wide, right, (((1,), (1,)), ((), ())), preferred_element_type=jnp.float32)
            total[r] += part.reshape(slabs, wide_b, near_b, rows, vb)

            if last:
                pl.when(i < away)(lambda: core_copy(r, step_c, order, to_c))
                pl.when(i >= away)(lambda: chip_copies(r, step_x, order, pair, to_x))

            return carry

        lax.fori_loop(0, pairs, one, 0)

    def amp_copy(m):
        to_k = lax.rem(my_k + m, kgrp)
        return pltpu.make_async_remote_copy(
            src_ref=amplitudes_ref,
            dst_ref=amps.at[pl.ds(my_k * per_group, per_group)],
            send_sem=amp_send,
            recv_sem=amp_recv,
            device_id=(to_k, my_b),
            device_id_type=MESH,
        )

    own_amp = pltpu.make_async_copy(amplitudes_ref, amps.at[pl.ds(my_k * per_group, per_group)], load_sem)

    def begin(p, carry):
        for h in range(split):
            if h:
                turn(p, h)
            else:
                pl.when(p > 0)(functools.partial(turn, p, h))
            if h + 1 < split:
                fetch_first(p, h + 1)
            else:
                pl.when(p + 1 < per_group)(functools.partial(fetch_first, p + 1, 0))

            def one(chunk, inner, h=h):
                pick_and_send(p, h, chunk)
                return inner

            lax.fori_loop(0, ahead, one, 0)
        return carry

    total[...] = jnp.zeros_like(total)
    turn(0, 0)
    for copy in tables:
        copy.wait()
    pl.semaphore_wait(barrier, devices - 1)
    lax.fori_loop(0, per_group, begin, 0)
    own_amp.start()
    for m in range(1, kgrp):
        amp_copy(m).start()
    own_amp.wait()
    all_amps = amps.at[pl.ds(0, (kgrp - 1) * per_group)]
    pltpu.make_async_copy(all_amps, all_amps, amp_send).wait()
    pltpu.make_async_copy(all_amps, all_amps, amp_recv).wait()

    def freed(chunk):
        slot = lax.rem(chunk, ahead)
        pltpu.make_async_copy(slots.at[slot], slots.at[slot], send_sem.at[slot]).wait()

    def main(chunk, carry):
        freed(chunk)

        @pl.when(chunk < chunks)
        def _():
            for p in range(per_group):
                pick_all(p, chunk)

        ladder(chunk - ahead)

        @pl.when(chunk < chunks - 1)
        def _():
            send_all(chunk, lambda ref: ref)

        @pl.when(chunk == chunks - 1)
        def _():
            send_all(chunk, head_of)
            send_all(chunk, tail_of, chunks)

        return carry

    lax.fori_loop(ahead, chunks + ahead - 1, main, 0)
    freed(chunks - 1)
    ladder(chunks - 1, 0, depth - 1)
    ladder(chunks - 1, depth - 1, 1, chunks, True)
    finish()


def fused(kgrp, band, densities, amplitudes, partner, qtable, grid_map, coulomb):
    per_group, rows, width, g_all = densities.shape
    slabs = amplitudes.shape[1]
    devices = kgrp * band
    pairs = kgrp * per_group
    vb = rows * band
    g_shard = g_all // devices
    depth = math.gcd(g_shard, DEPTH)
    chunks = g_shard // depth
    ahead = min(SLOTS, chunks - 1)
    span = math.gcd(g_all, 256)
    kind = densities.dtype
    anywhere = pl.BlockSpec(memory_space=pl.ANY)
    scalars = pl.BlockSpec(memory_space=pltpu.SMEM)
    split = math.gcd(max(rows // 8, 1), 2)
    part_rows = rows // split
    piece = (per_group, depth, split, part_rows, width)
    near_k, near_b = math.gcd(kgrp, 2), math.gcd(band, 2)
    wide_k, wide_b = kgrp // near_k, band // near_b
    half = wide_k * per_group
    spread = (slabs, wide_b, near_b, rows, vb)
    return pl.pallas_call(
        functools.partial(fused_kernel, kgrp, band),
        in_specs=[scalars, scalars, anywhere, anywhere, anywhere, anywhere],
        out_specs=[anywhere, pl.BlockSpec(memory_space=pltpu.VMEM)],
        out_shape=[
            jax.ShapeDtypeStruct((chunks, devices) + piece, kind),
            jax.ShapeDtypeStruct((rows, per_group, slabs, vb), kind),
        ],
        scratch_shapes=[
            pltpu.VMEM(grid_map.shape, grid_map.dtype),
            pltpu.VMEM(coulomb.shape, coulomb.dtype),
            pltpu.VMEM((per_group, g_all), grid_map.dtype),
            pltpu.VMEM((per_group, g_all), coulomb.dtype),
            pltpu.SMEM((per_group, g_all), grid_map.dtype),
            pltpu.SMEM((per_group, g_all), coulomb.dtype),
            pltpu.VMEM((per_group * g_all // span, span, split, part_rows, width), kind),
            pltpu.VMEM((STAGES, part_rows, width, span), kind),
            pltpu.VMEM((ahead, devices) + piece, kind),
            pltpu.VMEM((devices,) + piece, kind),
            pltpu.VMEM((pairs,) + amplitudes.shape[1:], kind),
            pltpu.VMEM((pairs,) + spread, jnp.float32),
            pltpu.VMEM((max(near_k - 1, 1), half) + spread, kind),
            pltpu.VMEM((max(near_k - 1, 1), half) + spread, kind),
            pltpu.VMEM((half, near_b, slabs, wide_b, rows, vb), kind),
            pltpu.VMEM((per_group, max(wide_k * near_b - 1, 1), slabs, wide_b, rows, vb), kind),
            pltpu.VMEM((per_group, max(wide_b - 1, 1), slabs, rows, vb), kind),
            pltpu.VMEM((per_group, max(wide_b - 1, 1), slabs, rows, vb), kind),
            pltpu.SemaphoreType.DMA((2,)),
            pltpu.SemaphoreType.DMA((STAGES,)),
            pltpu.SemaphoreType.DMA((ahead,)),
            pltpu.SemaphoreType.DMA((chunks + 1,)),
            pltpu.SemaphoreType.DMA,
            pltpu.SemaphoreType.DMA,
            pltpu.SemaphoreType.DMA,
            pltpu.SemaphoreType.DMA,
            pltpu.SemaphoreType.DMA((half,)),
            pltpu.SemaphoreType.DMA,
            pltpu.SemaphoreType.DMA((per_group,)),
            pltpu.SemaphoreType.DMA,
            pltpu.SemaphoreType.DMA((per_group,)),
        ],
        compiler_params=pltpu.CompilerParams(
            collective_id=0, has_side_effects=True, vmem_limit_bytes=67_043_328
        ),
        name="fused",
    )(partner, qtable, densities, amplitudes, grid_map, coulomb)


def shards(kgrp, band, densities, amplitudes, partner, qtable, grid_map, coulomb):
    return fused(kgrp, band, densities, amplitudes, partner, qtable, grid_map, coulomb)[1]


def solution(mesh):
    in_specs = (P("kgrp", "band", None, None), P("kgrp", None, None, None), P(), P(), P(), P())
    out_specs = P("band", "kgrp", None, None)
    body = functools.partial(shards, mesh.shape["kgrp"], mesh.shape["band"])
    return jax.shard_map(body, mesh=mesh, in_specs=in_specs, out_specs=out_specs, check_vma=False)
```
